32 devices in a mesh: hi: 4 (over x, core), lo: 8 (over z, y).
Axes of the slice: x: 2, y: 2, z: 4, core: 2. Of those that a mesh axis runs over, the one named last changes fastest.
Arguments:
- queries: bfloat16 [4096, 512], P(('hi', 'lo')), may hold values from -50 to 50
- key_rows: bfloat16 [4096, 128], P(('hi', 'lo')), may hold values from -6 to 6
- value_rows: bfloat16 [4096, 128], P(('hi', 'lo')), may hold values from -6 to 6
- global_positions: int32 [32, 8], P(('hi', 'lo')), may hold values from 0 to 127, as said below
Outputs:
- attended: bfloat16 [4096, 512], P(('hi', 'lo'))
The draws below stay inside these ranges and needn't reach their ends.
Inputs may be any that keep to these rules, and one draw needn't show every extreme that they name: `global_positions`: each row holds 8 distinct positions within a block.
All inputs are finite; a program needn't handle non-finite values.
Results may differ from the reference program's by a relative error of at most 0.0045.
Values may be sent and summed in bfloat16 or wider, within the bound.
A program may use at most 64 MiB of HBM per device.

```python
import jax
import jax.numpy as jnp
from jax import lax

H = 4
HD = 128
GLOB = 8
BLK = 128
NBLK = 32
TOKENS = 4096
N_HI = 4
N_LO = 8


def draw_key_rows(key, part):
    base = jax.random.fold_in(key, 11)
    rows = jnp.clip(jax.random.normal(base, (TOKENS, HD), jnp.float32), -6.0, 6.0)
    return rows.astype(jnp.bfloat16)


def draw_queries(key, part):
    base = jax.random.fold_in(key, 23)
    rows = 2.5 * jnp.clip(jax.random.normal(base, (TOKENS, H * HD), jnp.float32), -6.0, 6.0)
    return rows.astype(jnp.bfloat16)


def pick_slots(block_key):
    return jax.random.permutation(block_key, BLK)[:GLOB]


def draw_global_positions(key, part):
    base = jax.random.fold_in(key, 31)
    block_keys = jax.random.split(base, NBLK)
    return jax.vmap(pick_slots)(block_keys).astype(jnp.int32)


def shard_levels(own_key, shape, pieces, low, high):
    def one(position, parts):
        steps = jax.random.uniform(jax.random.fold_in(jax.random.fold_in(own_key, 6), position), (parts,), jnp.float32, low / len(pieces), high / len(pieces))
        return jnp.repeat(jnp.exp(steps), shape[position] // parts).reshape((-1,) + (1,) * (len(shape) - position - 1))

    loudness = one(*pieces[0])
    for cut in pieces[1:]:
        loudness = loudness * one(*cut)
    return loudness


def centred(rng, dims, deviation, bound, shards=(), kind=jnp.bfloat16):
    drawn = deviation * jax.random.normal(rng, dims, jnp.float32)
    if shards:
        drawn = drawn * shard_levels(rng, dims, shards, -0.22, 0.18)
    return jnp.clip(drawn, -bound, bound).astype(kind)


def setup_inputs(seed: int = 0) -> dict:
    seeds = jax.random.split(jax.random.key(seed), 5)
    queries = draw_queries(jax.random.fold_in(seeds[4], 71), 0)
    key_rows = draw_key_rows(jax.random.fold_in(seeds[4], 71), 0)
    value_rows = centred(seeds[2], (TOKENS, HD), 1.0, 6.0, ((0, 32),))
    global_positions = draw_global_positions(jax.random.fold_in(seeds[4], 71), 0)
    return {"queries": queries, "key_rows": key_rows, "value_rows": value_rows, "global_positions": global_positions}


def reference(queries, key_rows, value_rows, global_positions):
    block_count = N_HI * N_LO
    bit_count = block_count.bit_length() - 1
    starts = jnp.arange(block_count, dtype=jnp.int32)[:, None] * BLK
    flat_rows = (starts + global_positions.astype(jnp.int32)).reshape(-1)
    global_keys = jnp.take(key_rows, flat_rows, axis=0).astype(jnp.float32)
    global_values = jnp.take(value_rows, flat_rows, axis=0).astype(jnp.float32)
    blocked_keys = key_rows.reshape(block_count, BLK, HD).astype(jnp.float32)
    blocked_values = value_rows.reshape(block_count, BLK, HD).astype(jnp.float32)
    blocked_queries = queries.reshape(block_count, BLK, H, HD).astype(jnp.float32)

    def one_block(block_index):
        partner_list = [block_index] + [jnp.bitwise_xor(block_index, jnp.int32(1 << j)) for j in range(bit_count)]
        all_keys = jnp.concatenate([blocked_keys[p] for p in partner_list] + [global_keys], axis=0)
        all_values = jnp.concatenate([blocked_values[p] for p in partner_list] + [global_values], axis=0)
        scores = jnp.einsum("qhd,kd->hqk", blocked_queries[block_index], all_keys, precision=lax.Precision.HIGHEST) * (HD ** -0.5)
        row_peak = jnp.max(scores, axis=2, keepdims=True)
        raw_weights = jnp.exp(scores - row_peak)
        denominator = jnp.sum(raw_weights, axis=2)
        weights = lax.optimization_barrier(raw_weights.astype(jnp.bfloat16)).astype(jnp.float32)
        numerator = jnp.einsum("hqk,kd->qhd", weights, all_values, precision=lax.Precision.HIGHEST)
        result = numerator / jnp.transpose(denominator)[:, :, None]
        return result.reshape(BLK, H * HD).astype(jnp.bfloat16)

    attended = lax.map(one_block, jnp.arange(block_count, dtype=jnp.int32))
    return attended.reshape(TOKENS, H * HD)
```

```python
import functools
import math

import jax
import jax.numpy as jnp
from jax import lax
from jax.experimental import pallas as pl
from jax.experimental.pallas import tpu as pltpu
from jax.sharding import PartitionSpec as P

MESH = pl.DeviceIdType.MESH
GROUP_ROWS = 512


def dot(a, b, dims):
    return lax.dot_general(a, b, (dims, ((), ())), preferred_element_type=jnp.float32)


def attend(state, stacked, keys, values, factor):
    scores = dot(keys, stacked, ((1,), (1,)))
    fresh = jnp.max(scores, axis=0, keepdims=True)
    if state is not None:
        running, denominator, numerator = state
        fresh = jnp.maximum(running, fresh)
    weights = jnp.exp2((scores - fresh) * factor)
    total = jnp.sum(weights, axis=0, keepdims=True)
    update = dot(values, weights.astype(jnp.bfloat16), ((0,), (0,)))
    if state is not None:
        fade = jnp.exp2((running - fresh) * factor)
        total = denominator * fade + total
        update = numerator * fade + update
    return fresh, total, update


def flipped(index, bit):
    mask = 2**bit
    return index + mask - 2 * mask * lax.rem(lax.div(index, mask), 2)


def kernel(
    n_hi, n_lo, q_hbm, k_hbm, v_hbm, pos_hbm, out_ref,
    q, k, v, pos, slabs, k_in, v_in,
    local_sem, lo_send, lo_recv, hi_send, hi_recv, block_send, block_recv,
):
    hi, lo = lax.axis_index("hi"), lax.axis_index("lo")
    barrier = pltpu.get_barrier_semaphore()
    hi_peer = [lax.rem(hi + d, n_hi) for d in range(n_hi)]
    lo_peer = [lax.rem(lo + d, n_lo) for d in range(n_lo)]
    for d in range(1, n_lo):
        pl.semaphore_signal(barrier, inc=1, device_id={"lo": lo_peer[d]}, device_id_type=MESH)
    for d in range(1, n_hi):
        pl.semaphore_signal(barrier, inc=1, device_id={"hi": hi_peer[d]}, device_id_type=MESH)

    fetches = [
        pltpu.make_async_copy(source, target, local_sem.at[i])
        for i, (source, target) in enumerate(
            [(pos_hbm, pos), (k_hbm, k), (v_hbm, v), (q_hbm, q)]
        )
    ]
    for fetch in fetches:
        fetch.start()
    for fetch in fetches:
        fetch.wait()

    block_rows, width = k.shape
    heads = q.shape[1] // width
    glob = pos.shape[1]
    factor = width**-0.5 * math.log2(math.e)

    row = lax.broadcasted_iota(jnp.int32, (2 * glob, block_rows), 0)
    column = lax.broadcasted_iota(jnp.int32, (2 * glob, block_rows), 1)
    wanted = jnp.zeros_like(row)
    for i in range(glob):
        wanted = jnp.where(lax.rem(row, glob) == i, pos[0, i], wanted)
    one_hot = jnp.where(column == wanted, 1.0, 0.0).astype(jnp.bfloat16)
    picked_k = dot(one_hot, k[...], ((1,), (0,)))
    picked_v = dot(one_hot, v[...], ((1,), (0,)))
    top = lax.broadcasted_iota(jnp.int32, picked_k.shape, 0) < glob
    slabs[0, 0] = jnp.where(top, picked_k, picked_v).astype(jnp.bfloat16)

    stacked = jnp.concatenate([q[:, h * width : (h + 1) * width] for h in range(heads)], axis=0)
    state = attend(None, stacked, k[...], v[...], factor)

    pl.semaphore_wait(barrier, n_lo + n_hi - 2)

    lo_copies = []
    for d in range(1, n_lo):
        copy = pltpu.make_async_remote_copy(
            slabs.at[0, 0], slabs.at[0, d], lo_send.at[d], lo_recv.at[d],
            device_id={"lo": lo_peer[d]}, device_id_type=MESH,
        )
        copy.start()
        lo_copies.append(copy)

    def forward(d):
        for e in range(1, n_hi):
            pltpu.make_async_remote_copy(
                slabs.at[0, d], slabs.at[e, d], hi_send.at[e], hi_recv.at[e],
                device_id={"hi": hi_peer[e]}, device_id_type=MESH,
            ).start()

    forward(0)
    lo_bits, hi_bits = n_lo.bit_length() - 1, n_hi.bit_length() - 1
    partners = [("lo", b) for b in reversed(range(lo_bits))] + [("hi", b) for b in reversed(range(hi_bits))]
    blocks = []
    for j, (axis, bit) in enumerate(partners):
        target = {axis: flipped(lo if axis == "lo" else hi, bit)}
        for i, (source, place) in enumerate([(k, k_in), (v, v_in)]):
            copy = pltpu.make_async_remote_copy(
                source, place.at[j], block_send.at[i, j], block_recv.at[i, j],
                device_id=target, device_id_type=MESH,
            )
            copy.start()
            blocks.append(copy)

    for d in range(1, n_lo):
        lo_copies[d - 1].wait_recv()
        forward(d)

    near = len(partners) - 1
    for copy in blocks[2:]:
        copy.wait_recv()
    state = attend(
        state, stacked,
        k_in[1:].reshape(near * block_rows, width),
        v_in[1:].reshape(near * block_rows, width), factor,
    )

    for copy in blocks[:2]:
        copy.wait_recv()
    group = max(1, GROUP_ROWS // (n_lo * glob))
    for begin in range(0, n_hi, group):
        end = min(begin + group, n_hi)
        for e in range(max(begin, 1), end):
            pltpu.make_async_copy(slabs.at[e], slabs.at[e], hi_recv.at[e]).wait()
        mixed = slabs[begin:end].astype(jnp.float32)
        rows = (end - begin) * n_lo * glob
        keys = mixed[:, :, :glob].reshape(rows, width).astype(jnp.bfloat16)
        values = mixed[:, :, glob:].reshape(rows, width).astype(jnp.bfloat16)
        if begin == 0:
            keys = jnp.concatenate([k_in[0], keys], axis=0)
            values = jnp.concatenate([v_in[0], values], axis=0)
        state = attend(state, stacked, keys, values, factor)

    _, denominator, numerator = state
    result = numerator * (1.0 / denominator)
    for h in range(heads):
        part = result[:, h * block_rows : (h + 1) * block_rows]
        out_ref[:, h * width : (h + 1) * width] = jnp.transpose(part).astype(out_ref.dtype)

    for copy in lo_copies + blocks:
        copy.wait_send()
    for e in range(1, n_hi):
        pltpu.make_async_copy(slabs.at[e], slabs.at[e], hi_send.at[e]).wait()


def local(n_hi, n_lo, queries, key_rows, value_rows, global_positions):
    partners = (n_lo.bit_length() - 1) + (n_hi.bit_length() - 1)
    glob = global_positions.shape[1]
    width = key_rows.shape[1]
    dma = pltpu.SemaphoreType.DMA
    return pl.pallas_call(
        functools.partial(kernel, n_hi, n_lo),
        out_shape=jax.ShapeDtypeStruct(queries.shape, queries.dtype),
        in_specs=[pl.BlockSpec(memory_space=pl.ANY)] * 4,
        out_specs=pl.BlockSpec(memory_space=pltpu.VMEM),
        scratch_shapes=[
            pltpu.VMEM(queries.shape, queries.dtype),
            pltpu.VMEM(key_rows.shape, key_rows.dtype),
            pltpu.VMEM(value_rows.shape, value_rows.dtype),
            pltpu.SMEM(global_positions.shape, global_positions.dtype),
            pltpu.VMEM((n_hi, n_lo, 2 * glob, width), key_rows.dtype),
            pltpu.VMEM((partners,) + key_rows.shape, key_rows.dtype),
            pltpu.VMEM((partners,) + value_rows.shape, value_rows.dtype),
            dma((4,)),
            dma((n_lo,)),
            dma((n_lo,)),
            dma((n_hi,)),
            dma((n_hi,)),
            dma((2, partners)),
            dma((2, partners)),
        ],
        compiler_params=pltpu.CompilerParams(collective_id=0, has_side_effects=True),
    )(queries, key_rows, value_rows, global_positions)


def solution(mesh):
    spec = P(("hi", "lo"), None)
    return jax.shard_map(
        functools.partial(local, mesh.shape["hi"], mesh.shape["lo"]),
        mesh=mesh,
        in_specs=(spec,) * 4,
        out_specs=spec,
        check_vma=False,
    )
```

```python
import functools
import math

import jax
import jax.numpy as jnp
from jax import lax
from jax.experimental import pallas as pl
from jax.experimental.pallas import tpu as pltpu
from jax.sharding import PartitionSpec as P

MESH = pl.DeviceIdType.MESH
GROUP_ROWS = 512


def dot(a, b, dims):
    return lax.dot_general(a, b, (dims, ((), ())), preferred_element_type=jnp.float32)


def attend(state, stacked, keys, values, factor):
    scores = dot(keys, stacked, ((1,), (1,)))
    fresh = jnp.max(scores, axis=0, keepdims=True)
    if state is not None:
        running, denominator, numerator = state
        fresh = jnp.maximum(running, fresh)
    weights = jnp.exp2((scores - fresh) * factor)
    total = jnp.sum(weights, axis=0, keepdims=True)
    update = dot(values, weights.astype(jnp.bfloat16), ((0,), (0,)))
    if state is not None:
        fade = jnp.exp2((running - fresh) * factor)
        total = denominator * fade + total
        update = numerator * fade + update
    return fresh, total, update


def flipped(index, mask):
    bit = 1
    while bit <= mask:
        if mask & bit:
            index = index + bit - 2 * bit * lax.rem(lax.div(index, bit), 2)
        bit *= 2
    return index


def kernel(
    n_hi, n_lo, q_hbm, k_hbm, v_hbm, pos_hbm, out_ref,
    q, k, v, pos, slabs, k_in, v_in,
    local_sem, far_send, far_recv, near_send, near_recv, block_send, block_recv,
):
    hi, lo = lax.axis_index("hi"), lax.axis_index("lo")
    barrier = pltpu.get_barrier_semaphore()
    n_far, n_near = n_lo // 2, n_hi * 2
    far_peer = [{"lo": flipped(lo, 2 * f)} for f in range(n_far)]
    near_peer = [{"hi": flipped(hi, e // 2), "lo": flipped(lo, e % 2)} for e in range(n_near)]
    for peer in far_peer[1:] + near_peer[1:]:
        pl.semaphore_signal(barrier, inc=1, device_id=peer, device_id_type=MESH)

    fetches = [
        pltpu.make_async_copy(source, target, local_sem.at[i])
        for i, (source, target) in enumerate(
            [(pos_hbm, pos), (k_hbm, k), (v_hbm, v), (q_hbm, q)]
        )
    ]
    for fetch in fetches:
        fetch.start()
    for fetch in fetches:
        fetch.wait()

    block_rows, width = k.shape
    heads = q.shape[1] // width
    glob = pos.shape[1]
    factor = width**-0.5 * math.log2(math.e)

    row = lax.broadcasted_iota(jnp.int32, (2 * glob, block_rows), 0)
    column = lax.broadcasted_iota(jnp.int32, (2 * glob, block_rows), 1)
    wanted = jnp.zeros_like(row)
    for i in range(glob):
        wanted = jnp.where(lax.rem(row, glob) == i, pos[0, i], wanted)
    one_hot = jnp.where(column == wanted, 1.0, 0.0).astype(jnp.bfloat16)
    picked_k = dot(one_hot, k[...], ((1,), (0,)))
    picked_v = dot(one_hot, v[...], ((1,), (0,)))
    top = lax.broadcasted_iota(jnp.int32, picked_k.shape, 0) < glob
    slabs[0, 0] = jnp.where(top, picked_k, picked_v).astype(jnp.bfloat16)

    stacked = jnp.concatenate([q[:, h * width : (h + 1) * width] for h in range(heads)], axis=0)
    state = attend(None, stacked, k[...], v[...], factor)

    pl.semaphore_wait(barrier, n_far + n_near - 2)

    far_copies = []
    for f in range(1, n_far):
        copy = pltpu.make_async_remote_copy(
            slabs.at[0, 0], slabs.at[0, f], far_send.at[f], far_recv.at[f],
            device_id=far_peer[f], device_id_type=MESH,
        )
        copy.start()
        far_copies.append(copy)

    def forward(f):
        for e in range(1, n_near):
            pltpu.make_async_remote_copy(
                slabs.at[0, f], slabs.at[e, f], near_send.at[e], near_recv.at[e],
                device_id=near_peer[e], device_id_type=MESH,
            ).start()

    forward(0)
    lo_bits, hi_bits = n_lo.bit_length() - 1, n_hi.bit_length() - 1
    partners = [("lo", b) for b in reversed(range(lo_bits))] + [("hi", b) for b in reversed(range(hi_bits))]
    blocks = []
    for j, (axis, bit) in enumerate(partners):
        target = {axis: flipped(lo if axis == "lo" else hi, 2**bit)}
        for i, (source, place) in enumerate([(k, k_in), (v, v_in)]):
            copy = pltpu.make_async_remote_copy(
                source, place.at[j], block_send.at[i, j], block_recv.at[i, j],
                device_id=target, device_id_type=MESH,
            )
            copy.start()
            blocks.append(copy)

    for f in range(1, n_far):
        far_copies[f - 1].wait_recv()
        forward(f)

    near = len(partners) - 1
    for copy in blocks[2:]:
        copy.wait_recv()
    state = attend(
        state, stacked,
        k_in[1:].reshape(near * block_rows, width),
        v_in[1:].reshape(near * block_rows, width), factor,
    )

    for copy in blocks[:2]:
        copy.wait_recv()
    group = max(1, GROUP_ROWS // (n_far * glob))
    for begin in range(0, n_near, group):
        end = min(begin + group, n_near)
        for e in range(max(begin, 1), end):
            pltpu.make_async_copy(slabs.at[e], slabs.at[e], near_recv.at[e]).wait()
        mixed = slabs[begin:end].astype(jnp.float32)
        rows = (end - begin) * n_far * glob
        keys = mixed[:, :, :glob].reshape(rows, width).astype(jnp.bfloat16)
        values = mixed[:, :, glob:].reshape(rows, width).astype(jnp.bfloat16)
        if begin == 0:
            keys = jnp.concatenate([k_in[0], keys], axis=0)
            values = jnp.concatenate([v_in[0], values], axis=0)
        state = attend(state, stacked, keys, values, factor)

    _, denominator, numerator = state
    result = numerator * (1.0 / denominator)
    for h in range(heads):
        part = result[:, h * block_rows : (h + 1) * block_rows]
        out_ref[:, h * width : (h + 1) * width] = jnp.transpose(part).astype(out_ref.dtype)

    for copy in far_copies + blocks:
        copy.wait_send()
    for e in range(1, n_near):
        pltpu.make_async_copy(slabs.at[e], slabs.at[e], near_send.at[e]).wait()


def local(n_hi, n_lo, queries, key_rows, value_rows, global_positions):
    partners = (n_lo.bit_length() - 1) + (n_hi.bit_length() - 1)
    glob = global_positions.shape[1]
    width = key_rows.shape[1]
    dma = pltpu.SemaphoreType.DMA
    return pl.pallas_call(
        functools.partial(kernel, n_hi, n_lo),
        out_shape=jax.ShapeDtypeStruct(queries.shape, queries.dtype),
        in_specs=[pl.BlockSpec(memory_space=pltpu.HBM)] * 4,
        out_specs=pl.BlockSpec(memory_space=pltpu.VMEM),
        scratch_shapes=[
            pltpu.VMEM(queries.shape, queries.dtype),
            pltpu.VMEM(key_rows.shape, key_rows.dtype),
            pltpu.VMEM(value_rows.shape, value_rows.dtype),
            pltpu.SMEM(global_positions.shape, global_positions.dtype),
            pltpu.VMEM((2 * n_hi, n_lo // 2, 2 * glob, width), key_rows.dtype),
            pltpu.VMEM((partners,) + key_rows.shape, key_rows.dtype),
            pltpu.VMEM((partners,) + value_rows.shape, value_rows.dtype),
            dma((4,)),
            dma((n_lo // 2,)),
            dma((n_lo // 2,)),
            dma((2 * n_hi,)),
            dma((2 * n_hi,)),
            dma((2, partners)),
            dma((2, partners)),
        ],
        compiler_params=pltpu.CompilerParams(collective_id=0, has_side_effects=True, vmem_limit_bytes=12 * 2**20),
    )(*(pltpu.with_memory_space_constraint(x, pltpu.HBM) for x in (queries, key_rows, value_rows, global_positions)))


def solution(mesh):
    spec = P(("hi", "lo"), None)
    return jax.shard_map(
        functools.partial(local, mesh.shape["hi"], mesh.shape["lo"]),
        mesh=mesh,
        in_specs=(spec,) * 4,
        out_specs=spec,
        check_vma=False,
    )
```

```python
import functools
import math

import jax
import jax.numpy as jnp
from jax import lax
from jax.experimental import pallas as pl
from jax.experimental.pallas import tpu as pltpu
from jax.sharding import PartitionSpec as P

MESH = pl.DeviceIdType.MESH
GROUP_ROWS = 512


def dot(a, b, dims):
    return lax.dot_general(a, b, (dims, ((), ())), preferred_element_type=jnp.float32)


def attend(state, stacked, keys, values, factor):
    scores = dot(keys, stacked, ((1,), (1,)))
    fresh = jnp.max(scores, axis=0, keepdims=True)
    if state is not None:
        running, denominator, numerator = state
        fresh = jnp.maximum(running, fresh)
    weights = jnp.exp2((scores - fresh) * factor)
    total = jnp.sum(weights, axis=0, keepdims=True)
    update = dot(values, weights.astype(jnp.bfloat16), ((0,), (0,)))
    if state is not None:
        fade = jnp.exp2((running - fresh) * factor)
        total = denominator * fade + total
        update = numerator * fade + update
    return fresh, total, update


def flipped(index, mask):
    bit = 1
    while bit <= mask:
        if mask & bit:
            index = index + bit - 2 * bit * lax.rem(lax.div(index, bit), 2)
        bit *= 2
    return index


def kernel(
    n_hi, n_lo, q_hbm, k_hbm, v_hbm, pos_hbm, out_ref,
    q, k, v, pos, slabs, k_in, v_in,
    local_sem, far_send, far_recv, near_send, near_recv, block_send, block_recv,
):
    hi, lo = lax.axis_index("hi"), lax.axis_index("lo")
    barrier = pltpu.get_barrier_semaphore()
    n_far, n_near = n_lo // 2, n_hi * 2
    far_peer = [{"lo": flipped(lo, 2 * f)} for f in range(n_far)]
    near_peer = [{"hi": flipped(hi, e // 2), "lo": flipped(lo, e % 2)} for e in range(n_near)]
    for peer in far_peer[1:] + near_peer[1:]:
        pl.semaphore_signal(barrier, inc=1, device_id=peer, device_id_type=MESH)

    fetches = [
        pltpu.make_async_copy(source, target, local_sem.at[i])
        for i, (source, target) in enumerate(
            [(pos_hbm, pos), (k_hbm, k), (v_hbm, v), (q_hbm, q)]
        )
    ]
    for fetch in fetches:
        fetch.start()
    for fetch in fetches:
        fetch.wait()

    block_rows, width = k.shape
    heads = q.shape[1] // width
    glob = pos.shape[1]
    factor = width**-0.5 * math.log2(math.e)

    row = lax.broadcasted_iota(jnp.int32, (2 * glob, block_rows), 0)
    column = lax.broadcasted_iota(jnp.int32, (2 * glob, block_rows), 1)
    wanted = jnp.zeros_like(row)
    for i in range(glob):
        wanted = jnp.where(lax.rem(row, glob) == i, pos[0, i], wanted)
    one_hot = jnp.where(column == wanted, 1.0, 0.0).astype(jnp.bfloat16)
    picked_k = dot(one_hot, k[...], ((1,), (0,)))
    picked_v = dot(one_hot, v[...], ((1,), (0,)))
    top = lax.broadcasted_iota(jnp.int32, picked_k.shape, 0) < glob
    slabs[0, 0] = jnp.where(top, picked_k, picked_v).astype(jnp.bfloat16)

    stacked = jnp.concatenate([q[:, h * width : (h + 1) * width] for h in range(heads)], axis=0)
    state = attend(None, stacked, k[...], v[...], factor)

    pl.semaphore_wait(barrier, n_far + n_near - 2)

    far_copies = []
    for f in reversed(range(1, n_far)):
        copy = pltpu.make_async_remote_copy(
            slabs.at[0, 0], slabs.at[0, f], far_send.at[f], far_recv.at[f],
            device_id=far_peer[f], device_id_type=MESH,
        )
        copy.start()
        far_copies.insert(0, copy)

    def forward(f):
        for e in reversed(range(1, n_near)):
            pltpu.make_async_remote_copy(
                slabs.at[0, f], slabs.at[e, f], near_send.at[f], near_recv.at[f],
                device_id=near_peer[e], device_id_type=MESH,
            ).start()

    forward(0)
    lo_bits, hi_bits = n_lo.bit_length() - 1, n_hi.bit_length() - 1
    partners = [("lo", b) for b in reversed(range(lo_bits))] + [("hi", b) for b in reversed(range(hi_bits))]
    blocks = []
    for j, (axis, bit) in enumerate(partners):
        target = {axis: flipped(lo if axis == "lo" else hi, 2**bit)}
        for i, (source, place) in enumerate([(k, k_in), (v, v_in)]):
            copy = pltpu.make_async_remote_copy(
                source, place.at[j], block_send.at[i, j], block_recv.at[i, j],
                device_id=target, device_id_type=MESH,
            )
            copy.start()
            blocks.append(copy)

    for f in range(1, n_far):
        far_copies[f - 1].wait_recv()
        forward(f)

    for copy in blocks:
        copy.wait_recv()
    rows = len(partners) * block_rows
    state = attend(
        state, stacked, k_in[...].reshape(rows, width), v_in[...].reshape(rows, width), factor
    )

    group = max(1, GROUP_ROWS // (n_near * glob))
    cuts = list(range(0, n_far - 1, group)) + [n_far - 1, n_far]
    for begin, end in zip(cuts, cuts[1:]):
        for f in range(begin, end):
            pltpu.make_async_copy(slabs.at[1:, f], slabs.at[1:, f], near_recv.at[f]).wait()
        mixed = slabs[:, begin:end].astype(jnp.float32)
        rows = (end - begin) * n_near * glob
        keys = mixed[:, :, :glob].reshape(rows, width).astype(jnp.bfloat16)
        values = mixed[:, :, glob:].reshape(rows, width).astype(jnp.bfloat16)
        state = attend(state, stacked, keys, values, factor)

    _, denominator, numerator = state
    result = numerator * (1.0 / denominator)
    for h in range(heads):
        part = result[:, h * block_rows : (h + 1) * block_rows]
        out_ref[:, h * width : (h + 1) * width] = jnp.transpose(part).astype(out_ref.dtype)

    for copy in far_copies + blocks:
        copy.wait_send()
    for f in range(n_far):
        pltpu.make_async_copy(slabs.at[1:, f], slabs.at[1:, f], near_send.at[f]).wait()


def local(n_hi, n_lo, queries, key_rows, value_rows, global_positions):
    partners = (n_lo.bit_length() - 1) + (n_hi.bit_length() - 1)
    glob = global_positions.shape[1]
    width = key_rows.shape[1]
    dma = pltpu.SemaphoreType.DMA
    return pl.pallas_call(
        functools.partial(kernel, n_hi, n_lo),
        out_shape=jax.ShapeDtypeStruct(queries.shape, queries.dtype),
        in_specs=[pl.BlockSpec(memory_space=pltpu.HBM)] * 4,
        out_specs=pl.BlockSpec(memory_space=pltpu.VMEM),
        scratch_shapes=[
            pltpu.VMEM(queries.shape, queries.dtype),
            pltpu.VMEM(key_rows.shape, key_rows.dtype),
            pltpu.VMEM(value_rows.shape, value_rows.dtype),
            pltpu.SMEM(global_positions.shape, global_positions.dtype),
            pltpu.VMEM((2 * n_hi, n_lo // 2, 2 * glob, width), key_rows.dtype),
            pltpu.VMEM((partners,) + key_rows.shape, key_rows.dtype),
            pltpu.VMEM((partners,) + value_rows.shape, value_rows.dtype),
            dma((4,)),
            dma((n_lo // 2,)),
            dma((n_lo // 2,)),
            dma((n_lo // 2,)),
            dma((n_lo // 2,)),
            dma((2, partners)),
            dma((2, partners)),
        ],
        compiler_params=pltpu.CompilerParams(collective_id=0, has_side_effects=True, vmem_limit_bytes=12 * 2**20),
    )(*(pltpu.with_memory_space_constraint(x, pltpu.HBM) for x in (queries, key_rows, value_rows, global_positions)))


def solution(mesh):
    spec = P(("hi", "lo"), None)
    return jax.shard_map(
        functools.partial(local, mesh.shape["hi"], mesh.shape["lo"]),
        mesh=mesh,
        in_specs=(spec,) * 4,
        out_specs=spec,
        check_vma=False,
    )
```

```python
import functools
import math

import jax
import jax.numpy as jnp
from jax import lax
from jax.experimental import pallas as pl
from jax.experimental.pallas import tpu as pltpu
from jax.sharding import PartitionSpec as P

MESH = pl.DeviceIdType.MESH
GROUP_ROWS = 512


def dot(a, b, dims):
    return lax.dot_general(a, b, (dims, ((), ())), preferred_element_type=jnp.float32)


def attend(state, stacked, keys, values, factor):
    scores = dot(keys, stacked, ((1,), (1,)))
    fresh = jnp.max(scores, axis=0, keepdims=True)
    if state is not None:
        running, denominator, numerator = state
        fresh = jnp.maximum(running, fresh)
    weights = jnp.exp2((scores - fresh) * factor)
    total = jnp.sum(weights, axis=0, keepdims=True)
    update = dot(values, weights.astype(jnp.bfloat16), ((0,), (0,)))
    if state is not None:
        fade = jnp.exp2((running - fresh) * factor)
        total = denominator * fade + total
        update = numerator * fade + update
    return fresh, total, update


def flipped(index, mask):
    bit = 1
    while bit <= mask:
        if mask & bit:
            index = index + bit - 2 * bit * lax.rem(lax.div(index, bit), 2)
        bit *= 2
    return index


def kernel(
    n_hi, n_lo, q_hbm, k_hbm, v_hbm, pos_hbm, out_ref,
    q, k, v, pos, slabs, k_in, v_in,
    local_sem, far_send, far_recv, near_send, near_recv, block_send, block_recv,
):
    hi, lo = lax.axis_index("hi"), lax.axis_index("lo")
    barrier = pltpu.get_barrier_semaphore()
    n_far, n_near = n_lo // 2, n_hi * 2
    far_peer = [{"lo": flipped(lo, 2 * f)} for f in range(n_far)]
    near_peer = [{"hi": flipped(hi, e // 2), "lo": flipped(lo, e % 2)} for e in range(n_near)]
    for peer in far_peer[1:] + near_peer[1:]:
        pl.semaphore_signal(barrier, inc=1, device_id=peer, device_id_type=MESH)

    fetches = [
        pltpu.make_async_copy(source, target, local_sem.at[i])
        for i, (source, target) in enumerate(
            [(pos_hbm, pos), (k_hbm, k), (v_hbm, v), (q_hbm, q)]
        )
    ]
    for fetch in fetches:
        fetch.start()
    for fetch in fetches:
        fetch.wait()

    block_rows, width = k.shape
    heads = q.shape[1] // width
    glob = pos.shape[1]
    factor = width**-0.5 * math.log2(math.e)

    row = lax.broadcasted_iota(jnp.int32, (2 * glob, block_rows), 0)
    column = lax.broadcasted_iota(jnp.int32, (2 * glob, block_rows), 1)
    wanted = jnp.zeros_like(row)
    for i in range(glob):
        wanted = jnp.where(lax.rem(row, glob) == i, pos[0, i], wanted)
    one_hot = jnp.where(column == wanted, 1.0, 0.0).astype(jnp.bfloat16)
    picked_k = dot(one_hot, k[...], ((1,), (0,)))
    picked_v = dot(one_hot, v[...], ((1,), (0,)))
    top = lax.broadcasted_iota(jnp.int32, picked_k.shape, 0) < glob
    slabs[0, 0] = jnp.where(top, picked_k, picked_v).astype(jnp.bfloat16)

    stacked = jnp.concatenate([q[:, h * width : (h + 1) * width] for h in range(heads)], axis=0)
    state = attend(None, stacked, k[...], v[...], factor)

    pl.semaphore_wait(barrier, n_far + n_near - 2)

    far_copies = []
    for f in reversed(range(1, n_far)):
        copy = pltpu.make_async_remote_copy(
            slabs.at[0, 0], slabs.at[0, f], far_send.at[f], far_recv.at[f],
            device_id=far_peer[f], device_id_type=MESH,
        )
        copy.start()
        far_copies.insert(0, copy)

    def forward(f):
        for e in reversed(range(1, n_near)):
            pltpu.make_async_remote_copy(
                slabs.at[0, f], slabs.at[e, f], near_send.at[f], near_recv.at[f],
                device_id=near_peer[e], device_id_type=MESH,
            ).start()

    lo_bits, hi_bits = n_lo.bit_length() - 1, n_hi.bit_length() - 1
    partners = [("lo", b) for b in reversed(range(lo_bits))] + [("hi", b) for b in reversed(range(hi_bits))]
    blocks = []
    for j, (axis, bit) in enumerate(partners):
        target = {axis: flipped(lo if axis == "lo" else hi, 2**bit)}
        for i, (source, place) in enumerate([(k, k_in), (v, v_in)]):
            copy = pltpu.make_async_remote_copy(
                source, place.at[j], block_send.at[i, j], block_recv.at[i, j],
                device_id=target, device_id_type=MESH,
            )
            copy.start()
            blocks.append(copy)

    for f in range(n_far):
        if f:
            far_copies[f - 1].wait_recv()
        forward(f)

    for copy in blocks:
        copy.wait_recv()
    rows = len(partners) * block_rows
    state = attend(
        state, stacked, k_in[...].reshape(rows, width), v_in[...].reshape(rows, width), factor
    )

    group = max(1, GROUP_ROWS // (n_near * glob))
    cuts = list(range(0, n_far - 1, group)) + [n_far - 1, n_far]
    for begin, end in zip(cuts, cuts[1:]):
        for f in range(begin, end):
            pltpu.make_async_copy(slabs.at[1:, f], slabs.at[1:, f], near_recv.at[f]).wait()
        mixed = slabs[:, begin:end].astype(jnp.float32)
        rows = (end - begin) * n_near * glob
        keys = mixed[:, :, :glob].reshape(rows, width).astype(jnp.bfloat16)
        values = mixed[:, :, glob:].reshape(rows, width).astype(jnp.bfloat16)
        state = attend(state, stacked, keys, values, factor)

    _, denominator, numerator = state
    result = numerator * (1.0 / denominator)
    for h in range(heads):
        part = result[:, h * block_rows : (h + 1) * block_rows]
        out_ref[:, h * width : (h + 1) * width] = jnp.transpose(part).astype(out_ref.dtype)

    for copy in far_copies + blocks:
        copy.wait_send()
    for f in range(n_far):
        pltpu.make_async_copy(slabs.at[1:, f], slabs.at[1:, f], near_send.at[f]).wait()


def local(n_hi, n_lo, queries, key_rows, value_rows, global_positions):
    partners = (n_lo.bit_length() - 1) + (n_hi.bit_length() - 1)
    glob = global_positions.shape[1]
    width = key_rows.shape[1]
    dma = pltpu.SemaphoreType.DMA
    return pl.pallas_call(
        functools.partial(kernel, n_hi, n_lo),
        out_shape=jax.ShapeDtypeStruct(queries.shape, queries.dtype),
        in_specs=[pl.BlockSpec(memory_space=pltpu.HBM)] * 4,
        out_specs=pl.BlockSpec(memory_space=pltpu.VMEM),
        scratch_shapes=[
            pltpu.VMEM(queries.shape, queries.dtype),
            pltpu.VMEM(key_rows.shape, key_rows.dtype),
            pltpu.VMEM(value_rows.shape, value_rows.dtype),
            pltpu.SMEM(global_positions.shape, global_positions.dtype),
            pltpu.VMEM((2 * n_hi, n_lo // 2, 2 * glob, width), key_rows.dtype),
            pltpu.VMEM((partners,) + key_rows.shape, key_rows.dtype),
            pltpu.VMEM((partners,) + value_rows.shape, value_rows.dtype),
            dma((4,)),
            dma((n_lo // 2,)),
            dma((n_lo // 2,)),
            dma((n_lo // 2,)),
            dma((n_lo // 2,)),
            dma((2, partners)),
            dma((2, partners)),
        ],
        compiler_params=pltpu.CompilerParams(collective_id=0, has_side_effects=True, vmem_limit_bytes=12 * 2**20),
    )(*(pltpu.with_memory_space_constraint(x, pltpu.HBM) for x in (queries, key_rows, value_rows, global_positions)))


def solution(mesh):
    spec = P(("hi", "lo"), None)
    return jax.shard_map(
        functools.partial(local, mesh.shape["hi"], mesh.shape["lo"]),
        mesh=mesh,
        in_specs=(spec,) * 4,
        out_specs=spec,
        check_vma=False,
    )
```
